32 devices in a mesh: lat: 4 (over y, core), lon: 8 (over z, x).
Axes of the slice: x: 2, y: 2, z: 4, core: 2. Of those that a mesh axis runs over, the one named last changes fastest.
Arguments:
- night_field: float32 [24, 256, 2048], P(None, 'lat', 'lon'), may hold values from -6 to 6
- lat_kernel: float32 [24, 5], replicated, may hold values from 0.1 to 1
- lon_kernel: float32 [24, 5], replicated, may hold values from 0.1 to 1
- damping: float32 [4, 24], replicated, may hold values from 0.2 to 0.8
- observed: float32 [24, 8192], P(None, ('lat', 'lon')), may hold values from -6 to 6
- pixel_slot: int32 [256, 2048], P('lat', 'lon'), may hold values from 0 to 63, as said below
- inbox_district: int32 [32, 64], P(('lat', 'lon')), may hold values from 0 to 255
Outputs:
- back_field: float32 [24, 256, 2048], P(None, 'lat', 'lon')
- residual: float32 [24, 8192], P(None, ('lat', 'lon'))
The draws below stay inside these ranges and needn't reach their ends.
Inputs may be any that keep to these rules, and one draw needn't show every extreme that they name: `pixel_slot`: slot s of a device is sent to owner device s // 2, in the order latitude band first, then longitude strip. `inbox_district`: column source * 2 + k of an owner's row names the district, within the owner, of slot owner * 2 + k of that source device.
All inputs are finite; a program needn't handle non-finite values.
Results may differ from the reference program's by a relative error of at most 0.000068.
Values sent between devices are 32-bit elements; how exact they have to be, the bound alone decides.
A program may use at most 64 MiB of HBM per device.

```python
import jax
import jax.numpy as jnp
from jax import lax

CH = 24
TAPS = 5
PASSES = 4
ROWS = 64
COLS = 256
DBLK = 8
CAP = 2
DIST_DEV = 256
NLAT = 256
NLON = 2048
SLOTS = 64
DIST = 8192
N_LON = 8
DEVICES = 32


def draw_pixel_slot(key, part):
    first_key, second_key = jax.random.split(key)
    coarse = jax.random.randint(first_key, (NLAT // DBLK, NLON // DBLK), 0, SLOTS)
    blocked = jnp.repeat(jnp.repeat(coarse, DBLK, axis=0), DBLK, axis=1)
    shifted = jnp.roll(blocked, 1 + DBLK // 2, axis=1)
    chooser = jax.random.randint(second_key, (NLAT, NLON), 0, 4)
    chosen = jnp.where(chooser == 0, shifted, blocked)
    row_pos = jnp.arange(NLAT)[:, None] % ROWS
    col_pos = jnp.arange(NLON)[None, :] % COLS
    chosen = jnp.where((row_pos == 0) & (col_pos == 0), SLOTS - 1, chosen)
    chosen = jnp.where((row_pos == 0) & (col_pos == 1), 0, chosen)
    return chosen.astype(jnp.int32)


def plant(array, rng, smallest, top_value):
    longest = array.shape.index(max(array.shape))
    spots = []
    for shift in (0, 1):
        where = [jax.random.randint(jax.random.fold_in(rng, axis), (), 0, length) for axis, length in enumerate(array.shape)]
        where[longest] = (where[longest] + shift) % array.shape[longest]
        spots.append(tuple(where))
    return array.at[spots[0]].set(smallest).at[spots[1]].set(top_value)


def levels(stream_key, dims, shards, least, top_value):
    level = 1.0
    for dim, shards_of in shards:
        heights = jax.random.uniform(jax.random.fold_in(jax.random.fold_in(stream_key, 6), dim), (shards_of,), jnp.float32, least / len(shards), top_value / len(shards))
        level = level * jnp.repeat(jnp.exp(heights), dims[dim] // shards_of).reshape((-1,) + (1,) * (len(dims) - 1 - dim))
    return level


def noise(stream_key, shape, scale, bound, shards=(), kind=jnp.bfloat16):
    values = jax.random.normal(stream_key, shape, jnp.float32) * scale
    if len(shards) > 0:
        values = levels(stream_key, shape, shards, -0.22, 0.18) * values
    return jnp.clip(values, min=-bound, max=bound).astype(kind)


def setup_inputs(seed: int = 0) -> dict:
    seeds = jax.random.split(jax.random.key(seed), 8)
    night_field = noise(seeds[0], (CH, NLAT, NLON), 1.0, 6.0, ((1, 4), (2, 8)), jnp.float32)
    lat_kernel = jnp.clip(jax.random.uniform(seeds[1], (CH, TAPS), jnp.float32, 0.1, 1.0), 0.1, 1.0)
    lon_kernel = jnp.clip(jax.random.uniform(seeds[2], (CH, TAPS), jnp.float32, 0.1, 1.0), 0.1, 1.0)
    damping = jnp.clip(jax.random.uniform(seeds[3], (PASSES, CH), jnp.float32, 0.2, 0.8), 0.2, 0.8)
    observed = noise(seeds[4], (CH, DIST), 1.0, 6.0, ((1, 32),), jnp.float32)
    pixel_slot = draw_pixel_slot(jax.random.fold_in(seeds[7], 71), 0)
    inbox_district = plant(jax.random.randint(seeds[6], (DEVICES, SLOTS), 0, DIST_DEV), jax.random.fold_in(seeds[6], 1), 0, DIST_DEV - 1).astype(jnp.int32)
    return {"night_field": night_field, "lat_kernel": lat_kernel, "lon_kernel": lon_kernel, "damping": damping, "observed": observed, "pixel_slot": pixel_slot, "inbox_district": inbox_district}


def half_roll(values):
    return jnp.roll(values, NLON // 2, axis=-1)


def lon_pass(values, weights):
    summed = jnp.zeros_like(values)
    for offset in range(5):
        summed = summed + weights[offset] * jnp.roll(values, 2 - offset, axis=-1)
    return summed


def lat_pass(values, inner, outer):
    padded = jnp.pad(values, ((2, 2), (0, 0)))
    summed = jnp.zeros_like(values)
    for offset in range(5):
        summed = summed + inner[offset] * padded[offset:offset + NLAT]
    south = half_roll(values[:2])
    north = half_roll(values[-2:])
    summed = summed.at[0].add(outer[1] * south[0] + outer[0] * south[1])
    summed = summed.at[1].add(outer[0] * south[0])
    summed = summed.at[NLAT - 2].add(outer[4] * north[1])
    summed = summed.at[NLAT - 1].add(outer[3] * north[1] + outer[4] * north[0])
    return summed


def reference(night_field, lat_kernel, lon_kernel, damping, observed, pixel_slot, inbox_district):
    lat_taps = lat_kernel / jnp.sum(lat_kernel, axis=1, keepdims=True)
    lon_taps = lon_kernel / jnp.sum(lon_kernel, axis=1, keepdims=True)
    row_tile = (jnp.arange(NLAT, dtype=jnp.int32) // ROWS).astype(jnp.int32)
    col_tile = (jnp.arange(NLON, dtype=jnp.int32) // COLS).astype(jnp.int32)
    tile_index = (row_tile[:, None] * N_LON + col_tile[None, :]).astype(jnp.int32)
    owner = (pixel_slot // CAP).astype(jnp.int32)
    column = (tile_index * CAP + pixel_slot % CAP).astype(jnp.int32)
    district = (owner * DIST_DEV + inbox_district[owner, column]).astype(jnp.int32)
    flat_district = district.reshape(-1)
    sum_scale = (DIST_DEV / (ROWS * COLS)) ** 0.5

    def one_channel(channel_items):
        values, lat_one, lon_one, rates, wanted = channel_items
        for layer_index in range(PASSES):
            values = values - rates[layer_index] * lat_pass(lon_pass(values, lon_one), lat_one, lat_one)
        sums = jax.ops.segment_sum(values.reshape(-1), flat_district, num_segments=DIST)
        resid = sums * sum_scale - wanted
        spread = resid[flat_district].reshape(NLAT, NLON)
        for layer_index in range(PASSES):
            rate = rates[PASSES - 1 - layer_index]
            spread = spread - rate * lat_pass(lon_pass(spread, lon_one[::-1]), lat_one[::-1], lat_one)
        return spread, resid

    back_field, residual = lax.map(one_channel, (night_field, lat_taps, lon_taps, damping.T, observed))
    return back_field, residual
```

```python
import functools

import jax
import jax.numpy as jnp
from jax import lax
from jax.experimental import pallas as pl
from jax.experimental.pallas import tpu as pltpu
from jax.sharding import PartitionSpec as P

CAP = 2
HALO = 8
LANES = 128
GROUP = 16
BLOCK = 4
HIGHEST = lax.Precision.HIGHEST
MESH = pl.DeviceIdType.MESH
F32 = jnp.float32
BF16 = jnp.bfloat16
NT = (((1,), (1,)), ((), ()))


def fill_taps(lat_ref, lon_ref, damp_ref, lonw, latw, lat_here, lat_count, adjoint):
    channels = lat_ref.shape[0]
    lat_taps = lat_ref[...] / jnp.sum(lat_ref[...], axis=1, keepdims=True)
    lon_taps = lon_ref[...] / jnp.sum(lon_ref[...], axis=1, keepdims=True)
    layers = damp_ref.shape[0]

    def column(values, index):
        return jnp.broadcast_to(values[:, index : index + 1], (channels, LANES))

    lon_cols = [column(lon_taps, 4 - b if adjoint else b) for b in range(5)]
    lat_cols = [column(lat_taps, 4 - a if adjoint else a) for a in range(5)]
    for b in range(5):
        lonw[b] = lon_cols[b] / lon_cols[2]
    eye = lax.broadcasted_iota(jnp.int32, (channels, channels), 0) == lax.broadcasted_iota(
        jnp.int32, (channels, channels), 1
    )
    for k in range(layers):
        layer = layers - 1 - k if adjoint else k
        rates = jnp.broadcast_to(damp_ref[layer : layer + 1, :], (channels, channels))
        rate = jnp.sum(jnp.where(eye, rates, 0.0), axis=1, keepdims=True)
        scale = jnp.broadcast_to(rate, (channels, LANES)) * lon_cols[2]
        for a in range(5):
            own = scale * lat_cols[a]
            mirrored = scale * lat_cols[4 - a]
            latw[k, 0, a] = jnp.where(lat_here == 0, mirrored, own)
            latw[k, 1, a] = own
            latw[k, 2, a] = jnp.where(lat_here == lat_count - 1, mirrored, own)


def filter_pass(src, dst, lonw, latw, k, rows, last, adjoint):
    ext_rows, channels, width = src.shape
    keep = width - LANES if last else width
    first = 2 * (k + 1)
    blocks = (ext_rows - 2 * first) // BLOCK

    def wide(tap):
        return jnp.concatenate([tap] * (keep // LANES), axis=1)

    def group(g, _):
        chans = pl.ds(pl.multiple_of(g * 8, 8), 8)
        lon_taps = [wide(lonw[b, chans, :]) for b in range(5)]

        def lon(row):
            v = src[row, chans, :]
            total = v[:, :keep]
            for b in (0, 1, 3, 4):
                total = total + lon_taps[b] * pltpu.roll(v, (2 - b) % width, 1)[:, :keep]
            return total

        def step(i, carry):
            top = first + i * BLOCK
            t = list(carry) + [lon(top + 2 + j) for j in range(BLOCK)]
            for j in range(BLOCK):
                row = top + j
                out = src[row, chans, :keep]
                for a in range(5):
                    which = row + (a - 2) if adjoint else row
                    region = (which >= HALO).astype(jnp.int32) + (which >= HALO + rows).astype(jnp.int32)
                    out = out - wide(latw[k, region, a, chans, :]) * t[j + a]
                dst[row, chans, :keep] = out
            return tuple(t[BLOCK:])

        lax.fori_loop(0, blocks, step, tuple(lon(first - 2 + j) for j in range(4)))
        return 0

    lax.fori_loop(0, channels // 8, group, 0)


def run_passes(bufs, lonw, latw, layers, rows, adjoint):
    for k in range(layers):
        filter_pass(bufs[k % 2], bufs[(k + 1) % 2], lonw, latw, k, rows, k == layers - 1, adjoint)
    return bufs[layers % 2]


def pieces(values):
    high = values.astype(BF16).astype(F32)
    rest = values - high
    middle = rest.astype(BF16).astype(F32)
    return high, middle, rest - middle


def stacked(values, height):
    gap = jnp.zeros((32 - values.shape[0], values.shape[1]), F32)
    high, middle, low = pieces(values)
    parts = [high, gap, middle, gap, low, gap]
    if height > 96:
        parts.append(jnp.zeros((height - 96, values.shape[1]), F32))
    return jnp.concatenate(parts, axis=0).astype(BF16)


def slot_ids(devices, width):
    place = lax.broadcasted_iota(jnp.int32, (CAP * devices, width), 0)
    return jnp.where(place < devices, CAP * place, CAP * (place - devices) + 1)


def one_hot(slot_row, ids):
    return jnp.where(jnp.broadcast_to(slot_row, ids.shape) == ids, 1.0, 0.0).astype(BF16)


def unpack_rows(buf, right_of, left_of, corners_of, lat_here, lat_count, rows):
    channels, width = buf.shape[1], buf.shape[2]
    base = width - LANES
    lane = lax.broadcasted_iota(jnp.int32, (channels, LANES), 1)

    def place(row, right, left, i_right, i_left):
        a = pltpu.roll(right, i_right, 1)
        b = pltpu.roll(left, i_left, 1)
        zero = jnp.zeros_like(a)
        buf[row, :, base:] = jnp.where(lane < HALO, a, jnp.where(lane >= LANES - HALO, b, zero))

    def tile(p, _):
        right, left = right_of(p), left_of(p)
        for i in range(GROUP):
            place(
                HALO + p * GROUP + i, right, left, (-HALO * i) % LANES, (LANES - HALO - HALO * i) % LANES
            )
        return 0

    lax.fori_loop(0, rows // GROUP, tile, 0)
    for v in range(2):
        polar = (lat_here == 0) if v == 0 else (lat_here == lat_count - 1)
        right, left = corners_of(v, 1), corners_of(v, 0)
        for e in range(HALO):
            if v == 0:
                i = jnp.where(polar, HALO - 1 - e, HALO + e)
            else:
                i = jnp.where(polar, GROUP - 1 - e, e)
            row = e if v == 0 else HALO + rows + e
            place(
                row, right, left, (LANES - HALO * i) % LANES, (2 * LANES - HALO - HALO * i) % LANES
            )


def forward_kernel(
    lat_count, lon_count,
    x_ref, lat_ref, lon_ref, damp_ref, obs_ref, slot_ref, inbox_ref,
    resid_ref, nb_ref, srows_ref, sstrip_ref, scorner_ref,
    buf_a, buf_b, lonw, latw, pack, st_rows, st_slots, st_strip, st_corner,
    send_a, recv_a, send_b, recv_b, padded,
    near_send, near_recv, a_send, a_recv, b_send, b_recv,
):
    devices = lat_count * lon_count
    channels, rows, cols = x_ref.shape
    layers = damp_ref.shape[0]
    la, lo = lax.axis_index("lat"), lax.axis_index("lon")
    me = la * lon_count + lo
    half = lon_count // 2

    def coords(index):
        return (index // lon_count, lax.rem(index, lon_count))

    barrier = pltpu.get_barrier_semaphore()

    def greet(i, _):
        pl.semaphore_signal(
            barrier, inc=1, device_id=coords(lax.rem(me + i, devices)), device_id_type=MESH
        )
        return 0

    lax.fori_loop(1, devices, greet, 0)

    def turn(j, _):
        block = x_ref[:, pl.ds(pl.multiple_of(j * 8, 8), 8), :]
        buf_a[pl.ds(HALO + j * 8, 8), :, 0:cols] = jnp.swapaxes(block, 0, 1)
        return 0

    lax.fori_loop(0, rows // 8, turn, 0)

    lane_c = lax.broadcasted_iota(jnp.int32, (channels + 8, LANES), 1)

    def pack_tile(p, _):
        low = jnp.zeros((channels + 8, LANES), F32)
        high = low
        for i in range(GROUP):
            row = p * GROUP + i
            field = buf_a[HALO + row, :, :]
            slots = slot_ref[pl.ds(row, 1), :].astype(F32)
            first = jnp.concatenate(
                [field[:, :LANES], jnp.broadcast_to(slots[:, :LANES], (8, LANES))], axis=0
            )
            final = jnp.concatenate(
                [field[:, cols - LANES : cols], jnp.broadcast_to(slots[:, cols - LANES :], (8, LANES))],
                axis=0,
            )
            here = (lane_c >= HALO * i) & (lane_c < HALO * (i + 1))
            low = jnp.where(here, pltpu.roll(first, HALO * i, 1), low)
            high = jnp.where(here, pltpu.roll(final, (HALO * (i + 1)) % LANES, 1), high)
        pack[0, p] = low
        pack[1, p] = high
        return 0

    lax.fori_loop(0, rows // GROUP, pack_tile, 0)
    tiles = rows // GROUP

    left = lax.rem(lo + lon_count - 1, lon_count)
    right = lax.rem(lo + 1, lon_count)
    far = lax.rem(lo + half, lon_count)
    far_left = lax.rem(lo + half + lon_count - 1, lon_count)
    far_right = lax.rem(lo + half + 1, lon_count)
    south, north = la == 0, la == lat_count - 1
    up_lat, up_slot = jnp.where(south, la, la - 1), jnp.where(south, 0, 1)
    down_lat, down_slot = jnp.where(north, la, la + 1), jnp.where(north, 1, 0)

    def near(index, src, dst, place, target):
        return pltpu.make_async_remote_copy(
            src_ref=src, dst_ref=dst, send_sem=near_send.at[index], recv_sem=near_recv.at[place],
            device_id=target, device_id_type=MESH,
        )

    copies = []
    for v, lat_to, slot_to, polar in ((0, up_lat, up_slot, south), (1, down_lat, down_slot, north)):
        start = 0 if v == 0 else rows - HALO
        mid = (lat_to, jnp.where(polar, far, lo))
        copies.append(near(v, buf_a.at[pl.ds(HALO + start, HALO), :, pl.ds(0, cols)],
                           st_rows.at[slot_to], slot_to, mid))
        copies.append(near(2 + v, slot_ref.at[pl.ds(start, HALO)], st_slots.at[slot_to], 2 + slot_to, mid))
        edge = 0 if v == 0 else tiles - 1
        for side in range(2):
            side_lon = jnp.where(polar, far_left, left) if side == 0 else jnp.where(polar, far_right, right)
            copies.append(near(6 + 2 * v + side, pack.at[side, edge], st_corner.at[slot_to, 1 - side],
                               6 + 2 * slot_to + (1 - side), (lat_to, side_lon)))
    for side in range(2):
        copies.append(near(4 + side, pack.at[side], st_strip.at[1 - side], 4 + (1 - side),
                           (la, left if side == 0 else right)))

    pl.semaphore_wait(barrier, devices - 1)
    for copy in copies:
        copy.start()

    fill_taps(lat_ref, lon_ref, damp_ref, lonw, latw, la, lat_count, False)

    somewhere = (la, right)
    for v in range(2):
        near(v, st_rows.at[v], st_rows.at[v], v, somewhere).wait_recv()
        near(2 + v, st_slots.at[v], st_slots.at[v], 2 + v, somewhere).wait_recv()
        near(4 + v, st_strip.at[v], st_strip.at[v], 4 + v, somewhere).wait_recv()
        for h in range(2):
            near(6 + 2 * v + h, st_corner.at[v, h], st_corner.at[v, h], 6 + 2 * v + h, somewhere).wait_recv()
    for copy in copies:
        copy.wait_send()

    def ghost(e, _):
        for v in range(2):
            polar = south if v == 0 else north
            row = jnp.where(polar, HALO - 1 - e, e)
            buf_a[e + v * (HALO + rows), :, 0:cols] = st_rows[v, row]
        return 0

    lax.fori_loop(0, HALO, ghost, 0)
    srows_ref[...] = st_slots[...]
    sstrip_ref[...] = st_strip[:, :, channels:, :]
    scorner_ref[...] = st_corner[:, :, channels:, :]
    unpack_rows(
        buf_a,
        lambda p: st_strip[1, p, 0:channels, :],
        lambda p: st_strip[0, p, 0:channels, :],
        lambda v, h: st_corner[v, h, 0:channels, :],
        la, lat_count, rows,
    )

    done = run_passes((buf_a, buf_b), lonw, latw, layers, rows, False)

    ids = slot_ids(devices, cols)

    def add_row(row, total):
        block = stacked(done[HALO + row, :, 0:cols], LANES)
        hot = one_hot(slot_ref[pl.ds(row, 1), :], ids)
        return total + lax.dot_general(hot, block, NT, preferred_element_type=F32)

    sums = lax.fori_loop(0, rows, add_row, jnp.zeros((CAP * devices, LANES), F32))
    sums = sums + pltpu.roll(sums, LANES - 32, 1) + pltpu.roll(sums, LANES - 64, 1)
    lane_d = lax.broadcasted_iota(jnp.int32, (devices, LANES), 1)
    sums = jnp.where(lane_d < 64, sums[:devices], pltpu.roll(sums[devices:], 64, 1))
    send_a[...] = sums.reshape(devices, 1, LANES)

    def hand_out(i, _):
        to = lax.rem(me + i, devices)
        pltpu.make_async_remote_copy(
            src_ref=send_a.at[to], dst_ref=recv_a.at[me], send_sem=a_send, recv_sem=a_recv,
            device_id=coords(to), device_id_type=MESH,
        ).start()
        return 0

    lax.fori_loop(1, devices, hand_out, 0)
    recv_a[pl.ds(me, 1)] = send_a[pl.ds(me, 1)]

    districts = obs_ref.shape[1]
    place = lax.broadcasted_iota(jnp.int32, (devices, CAP * devices), 1)
    source = lax.broadcasted_iota(jnp.int32, (devices, CAP * devices), 0)
    inbox = jnp.broadcast_to(inbox_ref[...], (devices, CAP * devices)).astype(F32)
    number = lax.broadcasted_iota(jnp.int32, (devices, districts), 1)
    tables = []
    for k in range(CAP):
        wanted = jnp.sum(jnp.where(place == CAP * source + k, inbox, 0.0), axis=1, keepdims=True)
        wanted = jnp.broadcast_to(wanted.astype(jnp.int32), (devices, districts))
        tables.append(jnp.where(wanted == number, 1.0, 0.0))

    others = pl.ds(0, devices - 1)
    whole_a = pltpu.make_async_remote_copy(
        src_ref=send_a.at[others], dst_ref=recv_a.at[others], send_sem=a_send, recv_sem=a_recv,
        device_id=somewhere, device_id_type=MESH,
    )
    whole_a.wait_recv()
    turned = recv_a[...].reshape(devices, LANES).T
    held = jnp.zeros((channels, districts), F32)
    for k in range(CAP):
        held = held + jnp.dot(
            turned[64 * k : 64 * k + channels], tables[k], precision=HIGHEST, preferred_element_type=F32
        )
    resid = held * ((districts / (rows * cols)) ** 0.5) - obs_ref[...]
    resid_ref[...] = resid

    give = jnp.zeros((devices, LANES), F32)
    for k in range(CAP):
        parts = [resid, jnp.zeros((LANES - channels - 64 * k, districts), F32)]
        if k > 0:
            parts = [jnp.zeros((64 * k, districts), F32)] + parts
        give = give + lax.dot_general(
            tables[k], jnp.concatenate(parts, axis=0), NT, precision=HIGHEST, preferred_element_type=F32
        )
    send_b[...] = give.reshape(devices, 1, LANES)
    for ea in range(lat_count + 2):
        for eb in range(lon_count + 2):
            real = min(max(ea - 1, 0), lat_count - 1)
            shift = half if real != ea - 1 else 0
            padded[ea, eb] = send_b[real * lon_count + (eb - 1 + shift) % lon_count]

    def hand_back(i, _):
        to = lax.rem(me + i, devices)
        a, b = coords(to)
        pltpu.make_async_remote_copy(
            src_ref=padded.at[pl.ds(a, 3), pl.ds(b, 3)], dst_ref=recv_b.at[me],
            send_sem=b_send, recv_sem=b_recv, device_id=(a, b), device_id_type=MESH,
        ).start()
        return 0

    lax.fori_loop(1, devices, hand_back, 0)
    recv_b[me] = padded[pl.ds(la, 3), pl.ds(lo, 3)]
    whole_b = pltpu.make_async_remote_copy(
        src_ref=recv_b.at[others], dst_ref=recv_b.at[others], send_sem=b_send, recv_sem=b_recv,
        device_id=somewhere, device_id_type=MESH,
    )
    whole_b.wait_recv()
    nb_ref[...] = recv_b[...]
    whole_a.wait_send()
    whole_b.wait_send()


def adjoint_kernel(
    lat_count, lon_count,
    nb_ref, srows_ref, sstrip_ref, scorner_ref, slot_ref, lat_ref, lon_ref, damp_ref, where_ref,
    out_ref,
    buf_a, buf_b, lonw, latw, mixers, strips, corners,
):
    devices = lat_count * lon_count
    channels, rows, cols = out_ref.shape
    layers = damp_ref.shape[0]
    la = where_ref[0]
    fill_taps(lat_ref, lon_ref, damp_ref, lonw, latw, la, lat_count, True)
    for v in range(3):
        for h in range(3):
            turned = nb_ref[:, v, h, 0, :].T
            wide = jnp.concatenate([turned[0:channels], turned[64 : 64 + channels]], axis=1)
            mixers[v, h] = stacked(wide, 96)

    def mix(mixer, hot):
        made = jnp.dot(mixer, hot, preferred_element_type=F32)
        return made[0:channels] + made[32 : 32 + channels] + made[64 : 64 + channels]

    ids_strip = slot_ids(devices, LANES)
    for h in range(2):
        for p in range(rows // GROUP):
            strips[h, p] = mix(mixers[1, 2 * h], one_hot(sstrip_ref[h, p, 0:1, :].astype(jnp.int32), ids_strip))
        for v in range(2):
            corners[v, h] = mix(
                mixers[2 * v, 2 * h], one_hot(scorner_ref[v, h, 0:1, :].astype(jnp.int32), ids_strip)
            )
    ids = slot_ids(devices, cols)

    def own(row, _):
        buf_a[HALO + row, :, 0:cols] = mix(mixers[1, 1], one_hot(slot_ref[pl.ds(row, 1), :], ids))
        return 0

    lax.fori_loop(0, rows, own, 0)

    def ghost(e, _):
        for v in range(2):
            polar = (la == 0) if v == 0 else (la == lat_count - 1)
            row = jnp.where(polar, HALO - 1 - e, e)
            buf_a[e + v * (HALO + rows), :, 0:cols] = mix(
                mixers[2 * v, 1], one_hot(srows_ref[v, pl.ds(row, 1), :], ids)
            )
        return 0

    lax.fori_loop(0, HALO, ghost, 0)
    unpack_rows(
        buf_a, lambda p: strips[1, p], lambda p: strips[0, p], lambda v, h: corners[v, h],
        la, lat_count, rows,
    )
    done = run_passes((buf_a, buf_b), lonw, latw, layers, rows, True)

    def turn(j, _):
        block = done[pl.ds(HALO + j * 8, 8), :, 0:cols]
        out_ref[:, pl.ds(pl.multiple_of(j * 8, 8), 8), :] = jnp.swapaxes(block, 0, 1)
        return 0

    lax.fori_loop(0, rows // 8, turn, 0)


def local(night_field, lat_kernel, lon_kernel, damping, observed, pixel_slot, inbox_district):
    channels, rows, cols = night_field.shape
    layers = damping.shape[0]
    lat_count, lon_count = lax.axis_size("lat"), lax.axis_size("lon")
    devices = lat_count * lon_count
    districts = observed.shape[1]
    tiles = rows // GROUP
    ext = (rows + 2 * HALO, channels, cols + LANES)
    vmem = pl.BlockSpec(memory_space=pltpu.VMEM)
    shape = jax.ShapeDtypeStruct
    taps = [pltpu.VMEM((5, channels, LANES), F32), pltpu.VMEM((layers, 3, 5, channels, LANES), F32)]
    sem = pltpu.SemaphoreType.DMA
    residual, nb, srows, sstrip, scorner = pl.pallas_call(
        functools.partial(forward_kernel, lat_count, lon_count),
        out_shape=(
            shape((channels, districts), F32),
            shape((devices, 3, 3, 1, LANES), F32),
            shape((2, HALO, cols), jnp.int32),
            shape((2, tiles, 8, LANES), F32),
            shape((2, 2, 8, LANES), F32),
        ),
        in_specs=[vmem] * 7,
        out_specs=(vmem,) * 5,
        scratch_shapes=[
            pltpu.VMEM(ext, F32),
            pltpu.VMEM(ext, F32),
            *taps,
            pltpu.VMEM((2, tiles, channels + 8, LANES), F32),
            pltpu.VMEM((2, HALO, channels, cols), F32),
            pltpu.VMEM((2, HALO, cols), jnp.int32),
            pltpu.VMEM((2, tiles, channels + 8, LANES), F32),
            pltpu.VMEM((2, 2, channels + 8, LANES), F32),
            pltpu.VMEM((devices, 1, LANES), F32),
            pltpu.VMEM((devices, 1, LANES), F32),
            pltpu.VMEM((devices, 1, LANES), F32),
            pltpu.VMEM((devices, 3, 3, 1, LANES), F32),
            pltpu.VMEM((lat_count + 2, lon_count + 2, 1, LANES), F32),
            sem((10,)), sem((10,)), sem, sem, sem, sem,
        ],
        compiler_params=pltpu.CompilerParams(collective_id=0, has_side_effects=True),
    )(night_field, lat_kernel, lon_kernel, damping, observed, pixel_slot, inbox_district)
    here = lax.axis_index("lat").reshape(1).astype(jnp.int32)
    back_field = pl.pallas_call(
        functools.partial(adjoint_kernel, lat_count, lon_count),
        out_shape=shape((channels, rows, cols), F32),
        in_specs=[vmem] * 8 + [pl.BlockSpec(memory_space=pltpu.SMEM)],
        out_specs=vmem,
        scratch_shapes=[
            pltpu.VMEM(ext, F32),
            pltpu.VMEM(ext, F32),
            *taps,
            pltpu.VMEM((3, 3, 96, CAP * devices), BF16),
            pltpu.VMEM((2, tiles, channels, LANES), F32),
            pltpu.VMEM((2, 2, channels, LANES), F32),
        ],
    )(nb, srows, sstrip, scorner, pixel_slot, lat_kernel, lon_kernel, damping, here)
    return back_field, residual


def solution(mesh):
    placed = (
        P(None, "lat", "lon"),
        P(),
        P(),
        P(),
        P(None, ("lat", "lon")),
        P("lat", "lon"),
        P(("lat", "lon"), None),
    )
    return jax.shard_map(
        local,
        mesh=mesh,
        in_specs=placed,
        out_specs=(P(None, "lat", "lon"), P(None, ("lat", "lon"))),
        check_vma=False,
    )
```

```python
import functools

import jax
import jax.numpy as jnp
from jax import lax
from jax.experimental import pallas as pl
from jax.experimental.pallas import tpu as pltpu
from jax.sharding import PartitionSpec as P

CAP = 2
HALO = 8
LANES = 128
GROUP = 16
BLOCK = 4
HIGHEST = lax.Precision.HIGHEST
MESH = pl.DeviceIdType.MESH
F32 = jnp.float32
BF16 = jnp.bfloat16
NT = (((1,), (1,)), ((), ()))


def fill_taps(lat_ref, lon_ref, damp_ref, lonw, latw, lat_here, lat_count, adjoint):
    channels = lat_ref.shape[1]
    lat_taps = lat_ref[...] / jnp.sum(lat_ref[...], axis=0, keepdims=True)
    lon_taps = lon_ref[...] / jnp.sum(lon_ref[...], axis=0, keepdims=True)
    layers = damp_ref.shape[0]
    eye = lax.broadcasted_iota(jnp.int32, (channels, channels), 0) == lax.broadcasted_iota(
        jnp.int32, (channels, channels), 1
    )

    def column(values, index):
        wide = jnp.broadcast_to(values[index : index + 1, :], (channels, channels))
        tall = jnp.sum(jnp.where(eye, wide, 0.0), axis=1, keepdims=True)
        return jnp.broadcast_to(tall, (channels, LANES))

    lon_cols = [column(lon_taps, 4 - b if adjoint else b) for b in range(5)]
    lat_cols = [column(lat_taps, 4 - a if adjoint else a) for a in range(5)]
    for b in range(5):
        lonw[b] = lon_cols[b] / lon_cols[2]
    damping = damp_ref[...]
    for k in range(layers):
        scale = column(damping, layers - 1 - k if adjoint else k) * lon_cols[2]
        for a in range(5):
            own = scale * lat_cols[a]
            mirrored = scale * lat_cols[4 - a]
            latw[k, 0, a] = jnp.where(lat_here == 0, mirrored, own)
            latw[k, 1, a] = own
            latw[k, 2, a] = jnp.where(lat_here == lat_count - 1, mirrored, own)


def filter_pass(src, dst, tbufs, lonw, latw, k, rows, last, adjoint):
    ext_rows, channels, width = src.shape
    ring = width // LANES
    kept = ring - 1 if last else ring
    first = 2 * (k + 1)
    blocks = (ext_rows - 2 * first) // BLOCK
    lane = lax.broadcasted_iota(jnp.int32, (8, LANES), 1)
    groups = range(channels // 8)

    def lane_tile(n):
        return pl.ds(n * LANES, LANES)

    def lon(row, g):
        chans = pl.ds(g * 8, 8)
        v = [src[row, chans, lane_tile(n)] for n in range(ring)]
        totals = []
        for n in range(kept):
            before, after = v[(n - 1) % ring], v[(n + 1) % ring]
            total = v[n]
            for b in (0, 1, 3, 4):
                shift = 2 - b
                if shift > 0:
                    joined = jnp.where(lane >= LANES - shift, before, v[n])
                else:
                    joined = jnp.where(lane < -shift, after, v[n])
                total = total + lonw[b, chans, :] * pltpu.roll(joined, shift % LANES, 1)
            totals.append(total)
        return totals

    def keep_lon(row, g, totals):
        for n, total in enumerate(totals):
            tbufs[g][row, :, lane_tile(n)] = total

    def lat(top, g):
        chans = pl.ds(g * 8, 8)
        t = [[tbufs[g][top - 2 + j, :, lane_tile(n)] for n in range(kept)] for j in range(BLOCK + 4)]
        for j in range(BLOCK):
            row = top + j
            out = [src[row, chans, lane_tile(n)] for n in range(kept)]
            for a in range(5):
                which = row + (a - 2) if adjoint else row
                region = (which >= HALO) * 1 + (which >= HALO + rows) * 1
                tap = latw[k, region, a, chans, :]
                out = [out[n] - tap * t[j + a][n] for n in range(kept)]
            for n in range(kept):
                dst[row, chans, lane_tile(n)] = out[n]

    def begin(i, _):
        for g in groups:
            for j in range(BLOCK):
                row = first - 2 + i * BLOCK + j
                keep_lon(row, g, lon(row, g))
        return 0

    lax.fori_loop(0, 2, begin, 0)

    def step(i, _):
        top = first + i * BLOCK
        for g in groups:
            ahead = [lon(top + BLOCK + 2 + j, g) for j in range(BLOCK)]
            lat(top, g)
            for j in range(BLOCK):
                keep_lon(top + BLOCK + 2 + j, g, ahead[j])
        return 0

    lax.fori_loop(0, blocks - 1, step, 0)
    for g in groups:
        lat(first + (blocks - 1) * BLOCK, g)


def run_passes(bufs, tbufs, lonw, latw, layers, rows, adjoint):
    for k in range(layers):
        filter_pass(bufs[k % 2], bufs[(k + 1) % 2], tbufs, lonw, latw, k, rows, k == layers - 1, adjoint)
    return bufs[layers % 2]


def pieces(values):
    high = values.astype(BF16).astype(F32)
    rest = values - high
    middle = rest.astype(BF16).astype(F32)
    return high, middle, rest - middle


def stacked(values, height):
    gap = jnp.zeros((32 - values.shape[0], values.shape[1]), F32)
    high, middle, low = pieces(values)
    parts = [high, gap, middle, gap, low, gap]
    if height > 96:
        parts.append(jnp.zeros((height - 96, values.shape[1]), F32))
    return jnp.concatenate(parts, axis=0).astype(BF16)


def slot_ids(devices, width):
    place = lax.broadcasted_iota(jnp.int32, (CAP * devices, width), 0)
    return jnp.where(place < devices, CAP * place, CAP * (place - devices) + 1)


def one_hot(slot_row, ids):
    return jnp.where(jnp.broadcast_to(slot_row, ids.shape) == ids, 1.0, 0.0).astype(BF16)


def unpack_rows(buf, right_of, left_of, corners_of, lat_here, lat_count, rows):
    channels, width = buf.shape[1], buf.shape[2]
    base = width - LANES
    lane = lax.broadcasted_iota(jnp.int32, (channels, LANES), 1)

    def place(row, right, left, i_right, i_left):
        a = pltpu.roll(right, i_right, 1)
        b = pltpu.roll(left, i_left, 1)
        zero = jnp.zeros_like(a)
        buf[row, :, base:] = jnp.where(lane < HALO, a, jnp.where(lane >= LANES - HALO, b, zero))

    def tile(p, _):
        right, left = right_of(p), left_of(p)
        for i in range(GROUP):
            place(
                HALO + p * GROUP + i, right, left, (-HALO * i) % LANES, (LANES - HALO - HALO * i) % LANES
            )
        return 0

    lax.fori_loop(0, rows // GROUP, tile, 0)
    for v in range(2):
        polar = (lat_here == 0) if v == 0 else (lat_here == lat_count - 1)
        right, left = corners_of(v, 1), corners_of(v, 0)
        for e in range(HALO):
            if v == 0:
                i = jnp.where(polar, HALO - 1 - e, HALO + e)
            else:
                i = jnp.where(polar, GROUP - 1 - e, e)
            row = e if v == 0 else HALO + rows + e
            place(
                row, right, left, (LANES - HALO * i) % LANES, (2 * LANES - HALO - HALO * i) % LANES
            )


def forward_kernel(
    lat_count, lon_count,
    x_ref, lat_ref, lon_ref, damp_ref, obs_ref, slot_ref, inbox_ref,
    resid_ref, nb_ref, srows_ref, sstrip_ref, scorner_ref,
    buf_a, buf_b, tbuf_0, tbuf_1, tbuf_2, lonw, latw, pack, st_rows, st_slots, st_strip, st_corner,
    send_a, recv_a, send_b, recv_b, padded,
    near_send, near_recv, a_send, a_recv, b_send, b_recv,
):
    devices = lat_count * lon_count
    channels, rows, cols = x_ref.shape
    layers = damp_ref.shape[0]
    la, lo = lax.axis_index("lat"), lax.axis_index("lon")
    me = la * lon_count + lo
    half = lon_count // 2

    def coords(index):
        return (index // lon_count, lax.rem(index, lon_count))

    barrier = pltpu.get_barrier_semaphore()

    def greet(i, _):
        pl.semaphore_signal(
            barrier, inc=1, device_id=coords(lax.rem(me + i, devices)), device_id_type=MESH
        )
        return 0

    lax.fori_loop(1, devices, greet, 0)

    def turn(j, _):
        block = x_ref[:, pl.ds(pl.multiple_of(j * 8, 8), 8), :]
        buf_a[pl.ds(HALO + j * 8, 8), :, 0:cols] = jnp.swapaxes(block, 0, 1)
        return 0

    lax.fori_loop(0, rows // 8, turn, 0)

    lane_c = lax.broadcasted_iota(jnp.int32, (channels + 8, LANES), 1)

    def pack_tile(p, _):
        low = jnp.zeros((channels + 8, LANES), F32)
        high = low
        for i in range(GROUP):
            row = p * GROUP + i
            field = buf_a[HALO + row, :, :]
            slots = slot_ref[pl.ds(row, 1), :].astype(F32)
            first = jnp.concatenate(
                [field[:, :LANES], jnp.broadcast_to(slots[:, :LANES], (8, LANES))], axis=0
            )
            final = jnp.concatenate(
                [field[:, cols - LANES : cols], jnp.broadcast_to(slots[:, cols - LANES :], (8, LANES))],
                axis=0,
            )
            here = (lane_c >= HALO * i) & (lane_c < HALO * (i + 1))
            low = jnp.where(here, pltpu.roll(first, HALO * i, 1), low)
            high = jnp.where(here, pltpu.roll(final, (HALO * (i + 1)) % LANES, 1), high)
        pack[0, p] = low
        pack[1, p] = high
        return 0

    lax.fori_loop(0, rows // GROUP, pack_tile, 0)
    tiles = rows // GROUP

    left = lax.rem(lo + lon_count - 1, lon_count)
    right = lax.rem(lo + 1, lon_count)
    far = lax.rem(lo + half, lon_count)
    far_left = lax.rem(lo + half + lon_count - 1, lon_count)
    far_right = lax.rem(lo + half + 1, lon_count)
    south, north = la == 0, la == lat_count - 1
    up_lat, up_slot = jnp.where(south, la, la - 1), jnp.where(south, 0, 1)
    down_lat, down_slot = jnp.where(north, la, la + 1), jnp.where(north, 1, 0)

    def near(index, src, dst, place, target):
        return pltpu.make_async_remote_copy(
            src_ref=src, dst_ref=dst, send_sem=near_send.at[index], recv_sem=near_recv.at[place],
            device_id=target, device_id_type=MESH,
        )

    copies = []
    for v, lat_to, slot_to, polar in ((0, up_lat, up_slot, south), (1, down_lat, down_slot, north)):
        start = 0 if v == 0 else rows - HALO
        mid = (lat_to, jnp.where(polar, far, lo))
        copies.append(near(v, buf_a.at[pl.ds(HALO + start, HALO), :, pl.ds(0, cols)],
                           st_rows.at[slot_to], slot_to, mid))
        copies.append(near(2 + v, slot_ref.at[pl.ds(start, HALO)], st_slots.at[slot_to], 2 + slot_to, mid))
        edge = 0 if v == 0 else tiles - 1
        for side in range(2):
            side_lon = jnp.where(polar, far_left, left) if side == 0 else jnp.where(polar, far_right, right)
            copies.append(near(6 + 2 * v + side, pack.at[side, edge], st_corner.at[slot_to, 1 - side],
                               6 + 2 * slot_to + (1 - side), (lat_to, side_lon)))
    for side in range(2):
        copies.append(near(4 + side, pack.at[side], st_strip.at[1 - side], 4 + (1 - side),
                           (la, left if side == 0 else right)))

    pl.semaphore_wait(barrier, devices - 1)
    for copy in copies:
        copy.start()

    fill_taps(lat_ref, lon_ref, damp_ref, lonw, latw, la, lat_count, False)

    somewhere = (la, right)
    for v in range(2):
        near(v, st_rows.at[v], st_rows.at[v], v, somewhere).wait_recv()
        near(2 + v, st_slots.at[v], st_slots.at[v], 2 + v, somewhere).wait_recv()
        near(4 + v, st_strip.at[v], st_strip.at[v], 4 + v, somewhere).wait_recv()
        for h in range(2):
            near(6 + 2 * v + h, st_corner.at[v, h], st_corner.at[v, h], 6 + 2 * v + h, somewhere).wait_recv()
    for copy in copies:
        copy.wait_send()

    def ghost(e, _):
        for v in range(2):
            polar = south if v == 0 else north
            row = jnp.where(polar, HALO - 1 - e, e)
            buf_a[e + v * (HALO + rows), :, 0:cols] = st_rows[v, row]
        return 0

    lax.fori_loop(0, HALO, ghost, 0)
    srows_ref[...] = st_slots[...]
    sstrip_ref[...] = st_strip[:, :, channels:, :]
    scorner_ref[...] = st_corner[:, :, channels:, :]
    unpack_rows(
        buf_a,
        lambda p: st_strip[1, p, 0:channels, :],
        lambda p: st_strip[0, p, 0:channels, :],
        lambda v, h: st_corner[v, h, 0:channels, :],
        la, lat_count, rows,
    )

    done = run_passes((buf_a, buf_b), (tbuf_0, tbuf_1, tbuf_2), lonw, latw, layers, rows, False)

    ids = slot_ids(devices, cols)

    def add_row(row, total):
        block = stacked(done[HALO + row, :, 0:cols], LANES)
        hot = one_hot(slot_ref[pl.ds(row, 1), :], ids)
        return total + lax.dot_general(hot, block, NT, preferred_element_type=F32)

    sums = lax.fori_loop(0, rows, add_row, jnp.zeros((CAP * devices, LANES), F32))
    sums = sums + pltpu.roll(sums, LANES - 32, 1) + pltpu.roll(sums, LANES - 64, 1)
    lane_d = lax.broadcasted_iota(jnp.int32, (devices, LANES), 1)
    sums = jnp.where(lane_d < 64, sums[:devices], pltpu.roll(sums[devices:], 64, 1))
    send_a[...] = sums.reshape(devices, 1, LANES)

    def hand_out(i, _):
        to = lax.rem(me + i, devices)
        pltpu.make_async_remote_copy(
            src_ref=send_a.at[to], dst_ref=recv_a.at[me], send_sem=a_send, recv_sem=a_recv,
            device_id=coords(to), device_id_type=MESH,
        ).start()
        return 0

    lax.fori_loop(1, devices, hand_out, 0)
    recv_a[pl.ds(me, 1)] = send_a[pl.ds(me, 1)]

    districts = obs_ref.shape[1]
    place = lax.broadcasted_iota(jnp.int32, (devices, CAP * devices), 1)
    source = lax.broadcasted_iota(jnp.int32, (devices, CAP * devices), 0)
    inbox = jnp.broadcast_to(inbox_ref[...], (devices, CAP * devices)).astype(F32)
    number = lax.broadcasted_iota(jnp.int32, (devices, districts), 1)
    tables = []
    for k in range(CAP):
        wanted = jnp.sum(jnp.where(place == CAP * source + k, inbox, 0.0), axis=1, keepdims=True)
        wanted = jnp.broadcast_to(wanted.astype(jnp.int32), (devices, districts))
        tables.append(jnp.where(wanted == number, 1.0, 0.0))

    others = pl.ds(0, devices - 1)
    whole_a = pltpu.make_async_remote_copy(
        src_ref=send_a.at[others], dst_ref=recv_a.at[others], send_sem=a_send, recv_sem=a_recv,
        device_id=somewhere, device_id_type=MESH,
    )
    whole_a.wait_recv()
    turned = recv_a[...].reshape(devices, LANES).T
    held = jnp.zeros((channels, districts), F32)
    for k in range(CAP):
        held = held + jnp.dot(
            turned[64 * k : 64 * k + channels], tables[k], precision=HIGHEST, preferred_element_type=F32
        )
    resid = held * ((districts / (rows * cols)) ** 0.5) - obs_ref[...]
    resid_ref[...] = resid

    give = jnp.zeros((devices, LANES), F32)
    for k in range(CAP):
        parts = [resid, jnp.zeros((LANES - channels - 64 * k, districts), F32)]
        if k > 0:
            parts = [jnp.zeros((64 * k, districts), F32)] + parts
        give = give + lax.dot_general(
            tables[k], jnp.concatenate(parts, axis=0), NT, precision=HIGHEST, preferred_element_type=F32
        )
    send_b[...] = give.reshape(devices, 1, LANES)
    for ea in range(lat_count + 2):
        for eb in range(lon_count + 2):
            real = min(max(ea - 1, 0), lat_count - 1)
            shift = half if real != ea - 1 else 0
            padded[ea, eb] = send_b[real * lon_count + (eb - 1 + shift) % lon_count]

    def hand_back(i, _):
        to = lax.rem(me + i, devices)
        a, b = coords(to)
        pltpu.make_async_remote_copy(
            src_ref=padded.at[pl.ds(a, 3), pl.ds(b, 3)], dst_ref=recv_b.at[me],
            send_sem=b_send, recv_sem=b_recv, device_id=(a, b), device_id_type=MESH,
        ).start()
        return 0

    lax.fori_loop(1, devices, hand_back, 0)
    recv_b[me] = padded[pl.ds(la, 3), pl.ds(lo, 3)]
    whole_b = pltpu.make_async_remote_copy(
        src_ref=recv_b.at[others], dst_ref=recv_b.at[others], send_sem=b_send, recv_sem=b_recv,
        device_id=somewhere, device_id_type=MESH,
    )
    whole_b.wait_recv()
    nb_ref[...] = recv_b[...]
    whole_a.wait_send()
    whole_b.wait_send()


def adjoint_kernel(
    lat_count, lon_count,
    nb_ref, srows_ref, sstrip_ref, scorner_ref, slot_ref, lat_ref, lon_ref, damp_ref, where_ref,
    out_ref,
    buf_a, buf_b, tbuf_0, tbuf_1, tbuf_2, lonw, latw, mixers, strips, corners,
):
    devices = lat_count * lon_count
    channels, rows, cols = out_ref.shape
    layers = damp_ref.shape[0]
    la = where_ref[0]
    fill_taps(lat_ref, lon_ref, damp_ref, lonw, latw, la, lat_count, True)
    for v in range(3):
        for h in range(3):
            turned = nb_ref[:, v, h, 0, :].T
            wide = jnp.concatenate([turned[0:channels], turned[64 : 64 + channels]], axis=1)
            mixers[v, h] = stacked(wide, 96)

    def mix(mixer, hot):
        made = jnp.dot(mixer, hot, preferred_element_type=F32)
        return made[0:channels] + made[32 : 32 + channels] + made[64 : 64 + channels]

    ids_strip = slot_ids(devices, LANES)
    for h in range(2):
        for p in range(rows // GROUP):
            strips[h, p] = mix(mixers[1, 2 * h], one_hot(sstrip_ref[h, p, 0:1, :].astype(jnp.int32), ids_strip))
        for v in range(2):
            corners[v, h] = mix(
                mixers[2 * v, 2 * h], one_hot(scorner_ref[v, h, 0:1, :].astype(jnp.int32), ids_strip)
            )
    ids = slot_ids(devices, cols)

    def own(row, _):
        buf_a[HALO + row, :, 0:cols] = mix(mixers[1, 1], one_hot(slot_ref[pl.ds(row, 1), :], ids))
        return 0

    lax.fori_loop(0, rows, own, 0)

    def ghost(e, _):
        for v in range(2):
            polar = (la == 0) if v == 0 else (la == lat_count - 1)
            row = jnp.where(polar, HALO - 1 - e, e)
            buf_a[e + v * (HALO + rows), :, 0:cols] = mix(
                mixers[2 * v, 1], one_hot(srows_ref[v, pl.ds(row, 1), :], ids)
            )
        return 0

    lax.fori_loop(0, HALO, ghost, 0)
    unpack_rows(
        buf_a, lambda p: strips[1, p], lambda p: strips[0, p], lambda v, h: corners[v, h],
        la, lat_count, rows,
    )
    done = run_passes((buf_a, buf_b), (tbuf_0, tbuf_1, tbuf_2), lonw, latw, layers, rows, True)

    def turn(j, _):
        block = done[pl.ds(HALO + j * 8, 8), :, 0:cols]
        out_ref[:, pl.ds(pl.multiple_of(j * 8, 8), 8), :] = jnp.swapaxes(block, 0, 1)
        return 0

    lax.fori_loop(0, rows // 8, turn, 0)


def local(night_field, lat_kernel, lon_kernel, damping, observed, pixel_slot, inbox_district):
    channels, rows, cols = night_field.shape
    layers = damping.shape[0]
    lat_count, lon_count = lax.axis_size("lat"), lax.axis_size("lon")
    devices = lat_count * lon_count
    districts = observed.shape[1]
    tiles = rows // GROUP
    ext = (rows + 2 * HALO, channels, cols + LANES)
    sums = [pltpu.VMEM((ext[0], 8, ext[2]), F32)] * 3
    vmem = pl.BlockSpec(memory_space=pltpu.VMEM)
    shape = jax.ShapeDtypeStruct
    taps = [pltpu.VMEM((5, channels, LANES), F32), pltpu.VMEM((layers, 3, 5, channels, LANES), F32)]
    sem = pltpu.SemaphoreType.DMA
    residual, nb, srows, sstrip, scorner = pl.pallas_call(
        functools.partial(forward_kernel, lat_count, lon_count),
        out_shape=(
            shape((channels, districts), F32),
            shape((devices, 3, 3, 1, LANES), F32),
            shape((2, HALO, cols), jnp.int32),
            shape((2, tiles, 8, LANES), F32),
            shape((2, 2, 8, LANES), F32),
        ),
        in_specs=[vmem] * 7,
        out_specs=(vmem,) * 5,
        scratch_shapes=[
            pltpu.VMEM(ext, F32),
            pltpu.VMEM(ext, F32),
            *sums,
            *taps,
            pltpu.VMEM((2, tiles, channels + 8, LANES), F32),
            pltpu.VMEM((2, HALO, channels, cols), F32),
            pltpu.VMEM((2, HALO, cols), jnp.int32),
            pltpu.VMEM((2, tiles, channels + 8, LANES), F32),
            pltpu.VMEM((2, 2, channels + 8, LANES), F32),
            pltpu.VMEM((devices, 1, LANES), F32),
            pltpu.VMEM((devices, 1, LANES), F32),
            pltpu.VMEM((devices, 1, LANES), F32),
            pltpu.VMEM((devices, 3, 3, 1, LANES), F32),
            pltpu.VMEM((lat_count + 2, lon_count + 2, 1, LANES), F32),
            sem((10,)), sem((10,)), sem, sem, sem, sem,
        ],
        compiler_params=pltpu.CompilerParams(collective_id=0, has_side_effects=True),
    )(night_field, lat_kernel.T, lon_kernel.T, damping, observed, pixel_slot, inbox_district)
    here = lax.axis_index("lat").reshape(1).astype(jnp.int32)
    back_field = pl.pallas_call(
        functools.partial(adjoint_kernel, lat_count, lon_count),
        out_shape=shape((channels, rows, cols), F32),
        in_specs=[vmem] * 8 + [pl.BlockSpec(memory_space=pltpu.SMEM)],
        out_specs=vmem,
        scratch_shapes=[
            pltpu.VMEM(ext, F32),
            pltpu.VMEM(ext, F32),
            *sums,
            *taps,
            pltpu.VMEM((3, 3, 96, CAP * devices), BF16),
            pltpu.VMEM((2, tiles, channels, LANES), F32),
            pltpu.VMEM((2, 2, channels, LANES), F32),
        ],
    )(nb, srows, sstrip, scorner, pixel_slot, lat_kernel.T, lon_kernel.T, damping, here)
    return back_field, residual


def solution(mesh):
    placed = (
        P(None, "lat", "lon"),
        P(),
        P(),
        P(),
        P(None, ("lat", "lon")),
        P("lat", "lon"),
        P(("lat", "lon"), None),
    )
    return jax.shard_map(
        local,
        mesh=mesh,
        in_specs=placed,
        out_specs=(P(None, "lat", "lon"), P(None, ("lat", "lon"))),
        check_vma=False,
    )
```

```python
import functools

import jax
import jax.numpy as jnp
from jax import lax
from jax.experimental import pallas as pl
from jax.experimental.pallas import tpu as pltpu
from jax.sharding import PartitionSpec as P

CAP = 2
HALO = 8
LANES = 128
GROUP = 16
BLOCK = 4
HIGHEST = lax.Precision.HIGHEST
MESH = pl.DeviceIdType.MESH
F32 = jnp.float32
BF16 = jnp.bfloat16
NT = (((1,), (1,)), ((), ()))


def fill_taps(lat_ref, lon_ref, damp_ref, lonw, latw, lat_here, lat_count, adjoint):
    channels = lat_ref.shape[1]
    lat_taps = lat_ref[...] / jnp.sum(lat_ref[...], axis=0, keepdims=True)
    lon_taps = lon_ref[...] / jnp.sum(lon_ref[...], axis=0, keepdims=True)
    layers = damp_ref.shape[0]
    eye = lax.broadcasted_iota(jnp.int32, (channels, channels), 0) == lax.broadcasted_iota(
        jnp.int32, (channels, channels), 1
    )

    def column(values, index):
        wide = jnp.broadcast_to(values[index : index + 1, :], (channels, channels))
        tall = jnp.sum(jnp.where(eye, wide, 0.0), axis=1, keepdims=True)
        return jnp.broadcast_to(tall, (channels, LANES))

    lon_cols = [column(lon_taps, 4 - b if adjoint else b) for b in range(5)]
    lat_cols = [column(lat_taps, 4 - a if adjoint else a) for a in range(5)]
    for b in range(5):
        lonw[b] = lon_cols[b] / lon_cols[2]
    damping = damp_ref[...]
    for k in range(layers):
        scale = column(damping, layers - 1 - k if adjoint else k) * lon_cols[2]
        for a in range(5):
            own = scale * lat_cols[a]
            mirrored = scale * lat_cols[4 - a]
            latw[k, 0, a] = jnp.where(lat_here == 0, mirrored, own)
            latw[k, 1, a] = own
            latw[k, 2, a] = jnp.where(lat_here == lat_count - 1, mirrored, own)


def filter_pass(src, dst, tbufs, lonw, latw, k, rows, last, adjoint):
    ext_rows, channels, width = src.shape
    ring = width // LANES
    kept = ring - 1 if last else ring
    first = 2 * (k + 1)
    blocks = (ext_rows - 2 * first) // BLOCK
    lane = lax.broadcasted_iota(jnp.int32, (8, LANES), 1)
    groups = range(channels // 8)

    def lane_tile(n):
        return pl.ds(n * LANES, LANES)

    def lon(row, g):
        chans = pl.ds(g * 8, 8)
        v = [src[row, chans, lane_tile(n)] for n in range(ring)]
        totals = []
        for n in range(kept):
            before, after = v[(n - 1) % ring], v[(n + 1) % ring]
            total = v[n]
            for b in (0, 1, 3, 4):
                shift = 2 - b
                if shift > 0:
                    joined = jnp.where(lane >= LANES - shift, before, v[n])
                else:
                    joined = jnp.where(lane < -shift, after, v[n])
                total = total + lonw[b, chans, :] * pltpu.roll(joined, shift % LANES, 1)
            totals.append(total)
        return totals

    def keep_lon(row, g, totals):
        for n, total in enumerate(totals):
            tbufs[g][row, :, lane_tile(n)] = total

    def lat(top, g):
        chans = pl.ds(g * 8, 8)
        t = [[tbufs[g][top - 2 + j, :, lane_tile(n)] for n in range(kept)] for j in range(BLOCK + 4)]
        for j in range(BLOCK):
            row = top + j
            out = [src[row, chans, lane_tile(n)] for n in range(kept)]
            for a in range(5):
                which = row + (a - 2) if adjoint else row
                region = (which >= HALO) * 1 + (which >= HALO + rows) * 1
                tap = latw[k, region, a, chans, :]
                out = [out[n] - tap * t[j + a][n] for n in range(kept)]
            for n in range(kept):
                dst[row, chans, lane_tile(n)] = out[n]

    def begin(i, _):
        for g in groups:
            for j in range(BLOCK):
                row = first - 2 + i * BLOCK + j
                keep_lon(row, g, lon(row, g))
        return 0

    lax.fori_loop(0, 2, begin, 0)

    def step(i, _):
        top = first + i * BLOCK
        for g in groups:
            ahead = [lon(top + BLOCK + 2 + j, g) for j in range(BLOCK)]
            lat(top, g)
            for j in range(BLOCK):
                keep_lon(top + BLOCK + 2 + j, g, ahead[j])
        return 0

    def two_steps(i, _):
        step(2 * i, 0)
        return step(2 * i + 1, 0)

    lax.fori_loop(0, (blocks - 1) // 2, two_steps, 0)
    if (blocks - 1) % 2:
        step(blocks - 2, 0)
    for g in groups:
        lat(first + (blocks - 1) * BLOCK, g)


def run_passes(bufs, tbufs, lonw, latw, layers, rows, adjoint):
    for k in range(layers):
        filter_pass(bufs[k % 2], bufs[(k + 1) % 2], tbufs, lonw, latw, k, rows, k == layers - 1, adjoint)
    return bufs[layers % 2]


def pieces(values):
    high = values.astype(BF16).astype(F32)
    rest = values - high
    middle = rest.astype(BF16).astype(F32)
    return high, middle, rest - middle


def stacked(values, height):
    gap = jnp.zeros((32 - values.shape[0], values.shape[1]), F32)
    high, middle, low = pieces(values)
    parts = [high, gap, middle, gap, low, gap]
    if height > 96:
        parts.append(jnp.zeros((height - 96, values.shape[1]), F32))
    return jnp.concatenate(parts, axis=0).astype(BF16)


def slot_ids(devices, width):
    place = lax.broadcasted_iota(jnp.int32, (CAP * devices, width), 0)
    return jnp.where(place < devices, CAP * place, CAP * (place - devices) + 1)


def one_hot(slot_row, ids):
    return jnp.where(jnp.broadcast_to(slot_row, ids.shape) == ids, 1.0, 0.0).astype(BF16)


def unpack_rows(buf, right_of, left_of, corners_of, lat_here, lat_count, rows):
    channels, width = buf.shape[1], buf.shape[2]
    base = width - LANES
    lane = lax.broadcasted_iota(jnp.int32, (channels, LANES), 1)

    def place(row, right, left, i_right, i_left):
        a = pltpu.roll(right, i_right, 1)
        b = pltpu.roll(left, i_left, 1)
        zero = jnp.zeros_like(a)
        buf[row, :, base:] = jnp.where(lane < HALO, a, jnp.where(lane >= LANES - HALO, b, zero))

    def tile(p, _):
        right, left = right_of(p), left_of(p)
        for i in range(GROUP):
            place(
                HALO + p * GROUP + i, right, left, (-HALO * i) % LANES, (LANES - HALO - HALO * i) % LANES
            )
        return 0

    lax.fori_loop(0, rows // GROUP, tile, 0)
    for v in range(2):
        polar = (lat_here == 0) if v == 0 else (lat_here == lat_count - 1)
        right, left = corners_of(v, 1), corners_of(v, 0)
        for e in range(HALO):
            if v == 0:
                i = jnp.where(polar, HALO - 1 - e, HALO + e)
            else:
                i = jnp.where(polar, GROUP - 1 - e, e)
            row = e if v == 0 else HALO + rows + e
            place(
                row, right, left, (LANES - HALO * i) % LANES, (2 * LANES - HALO - HALO * i) % LANES
            )


def forward_kernel(
    lat_count, lon_count,
    x_ref, lat_ref, lon_ref, damp_ref, obs_ref, slot_ref, inbox_ref,
    resid_ref, nb_ref, srows_ref, sstrip_ref, scorner_ref,
    buf_a, buf_b, tbuf_0, tbuf_1, tbuf_2, lonw, latw, pack, st_rows, st_slots, st_strip, st_corner,
    send_a, recv_a, send_b, recv_b, padded,
    near_send, near_recv, a_send, a_recv, b_send, b_recv,
):
    devices = lat_count * lon_count
    channels, rows, cols = x_ref.shape
    layers = damp_ref.shape[0]
    la, lo = lax.axis_index("lat"), lax.axis_index("lon")
    me = la * lon_count + lo
    half = lon_count // 2

    def coords(index):
        return (index // lon_count, lax.rem(index, lon_count))

    barrier = pltpu.get_barrier_semaphore()

    def greet(i, _):
        pl.semaphore_signal(
            barrier, inc=1, device_id=coords(lax.rem(me + i, devices)), device_id_type=MESH
        )
        return 0

    lax.fori_loop(1, devices, greet, 0)

    def turn(j, _):
        block = x_ref[:, pl.ds(pl.multiple_of(j * 8, 8), 8), :]
        buf_a[pl.ds(HALO + j * 8, 8), :, 0:cols] = jnp.swapaxes(block, 0, 1)
        return 0

    lax.fori_loop(0, rows // 8, turn, 0)

    lane_c = lax.broadcasted_iota(jnp.int32, (channels + 8, LANES), 1)

    def pack_tile(p, _):
        low = jnp.zeros((channels + 8, LANES), F32)
        high = low
        for i in range(GROUP):
            row = p * GROUP + i
            field = buf_a[HALO + row, :, :]
            slots = slot_ref[pl.ds(row, 1), :].astype(F32)
            first = jnp.concatenate(
                [field[:, :LANES], jnp.broadcast_to(slots[:, :LANES], (8, LANES))], axis=0
            )
            final = jnp.concatenate(
                [field[:, cols - LANES : cols], jnp.broadcast_to(slots[:, cols - LANES :], (8, LANES))],
                axis=0,
            )
            here = (lane_c >= HALO * i) & (lane_c < HALO * (i + 1))
            low = jnp.where(here, pltpu.roll(first, HALO * i, 1), low)
            high = jnp.where(here, pltpu.roll(final, (HALO * (i + 1)) % LANES, 1), high)
        pack[0, p] = low
        pack[1, p] = high
        return 0

    lax.fori_loop(0, rows // GROUP, pack_tile, 0)
    tiles = rows // GROUP

    left = lax.rem(lo + lon_count - 1, lon_count)
    right = lax.rem(lo + 1, lon_count)
    far = lax.rem(lo + half, lon_count)
    far_left = lax.rem(lo + half + lon_count - 1, lon_count)
    far_right = lax.rem(lo + half + 1, lon_count)
    south, north = la == 0, la == lat_count - 1
    up_lat, up_slot = jnp.where(south, la, la - 1), jnp.where(south, 0, 1)
    down_lat, down_slot = jnp.where(north, la, la + 1), jnp.where(north, 1, 0)

    def near(index, src, dst, place, target):
        return pltpu.make_async_remote_copy(
            src_ref=src, dst_ref=dst, send_sem=near_send.at[index], recv_sem=near_recv.at[place],
            device_id=target, device_id_type=MESH,
        )

    copies = []
    for v, lat_to, slot_to, polar in ((0, up_lat, up_slot, south), (1, down_lat, down_slot, north)):
        start = 0 if v == 0 else rows - HALO
        mid = (lat_to, jnp.where(polar, far, lo))
        copies.append(near(v, buf_a.at[pl.ds(HALO + start, HALO), :, pl.ds(0, cols)],
                           st_rows.at[slot_to], slot_to, mid))
        copies.append(near(2 + v, slot_ref.at[pl.ds(start, HALO)], st_slots.at[slot_to], 2 + slot_to, mid))
        edge = 0 if v == 0 else tiles - 1
        for side in range(2):
            side_lon = jnp.where(polar, far_left, left) if side == 0 else jnp.where(polar, far_right, right)
            copies.append(near(6 + 2 * v + side, pack.at[side, edge], st_corner.at[slot_to, 1 - side],
                               6 + 2 * slot_to + (1 - side), (lat_to, side_lon)))
    for side in range(2):
        copies.append(near(4 + side, pack.at[side], st_strip.at[1 - side], 4 + (1 - side),
                           (la, left if side == 0 else right)))

    pl.semaphore_wait(barrier, devices - 1)
    for copy in copies:
        copy.start()

    fill_taps(lat_ref, lon_ref, damp_ref, lonw, latw, la, lat_count, False)

    somewhere = (la, right)
    for v in range(2):
        near(v, st_rows.at[v], st_rows.at[v], v, somewhere).wait_recv()
        near(2 + v, st_slots.at[v], st_slots.at[v], 2 + v, somewhere).wait_recv()
        near(4 + v, st_strip.at[v], st_strip.at[v], 4 + v, somewhere).wait_recv()
        for h in range(2):
            near(6 + 2 * v + h, st_corner.at[v, h], st_corner.at[v, h], 6 + 2 * v + h, somewhere).wait_recv()
    for copy in copies:
        copy.wait_send()

    def ghost(e, _):
        for v in range(2):
            polar = south if v == 0 else north
            row = jnp.where(polar, HALO - 1 - e, e)
            buf_a[e + v * (HALO + rows), :, 0:cols] = st_rows[v, row]
        return 0

    lax.fori_loop(0, HALO, ghost, 0)
    srows_ref[...] = st_slots[...]
    sstrip_ref[...] = st_strip[:, :, channels:, :]
    scorner_ref[...] = st_corner[:, :, channels:, :]
    unpack_rows(
        buf_a,
        lambda p: st_strip[1, p, 0:channels, :],
        lambda p: st_strip[0, p, 0:channels, :],
        lambda v, h: st_corner[v, h, 0:channels, :],
        la, lat_count, rows,
    )

    done = run_passes((buf_a, buf_b), (tbuf_0, tbuf_1, tbuf_2), lonw, latw, layers, rows, False)

    ids = slot_ids(devices, cols)

    def add_rows(i, total):
        for j in range(4):
            row = 4 * i + j
            block = stacked(done[HALO + row, :, 0:cols], LANES)
            hot = one_hot(slot_ref[pl.ds(row, 1), :], ids)
            total = total + lax.dot_general(hot, block, NT, preferred_element_type=F32)
        return total

    sums = lax.fori_loop(0, rows // 4, add_rows, jnp.zeros((CAP * devices, LANES), F32))
    sums = sums + pltpu.roll(sums, LANES - 32, 1) + pltpu.roll(sums, LANES - 64, 1)
    lane_d = lax.broadcasted_iota(jnp.int32, (devices, LANES), 1)
    sums = jnp.where(lane_d < 64, sums[:devices], pltpu.roll(sums[devices:], 64, 1))
    send_a[...] = sums.reshape(devices, 1, LANES)

    def hand_out(i, _):
        to = lax.rem(me + i, devices)
        pltpu.make_async_remote_copy(
            src_ref=send_a.at[to], dst_ref=recv_a.at[me], send_sem=a_send, recv_sem=a_recv,
            device_id=coords(to), device_id_type=MESH,
        ).start()
        return 0

    lax.fori_loop(1, devices, hand_out, 0)
    recv_a[pl.ds(me, 1)] = send_a[pl.ds(me, 1)]

    districts = obs_ref.shape[1]
    place = lax.broadcasted_iota(jnp.int32, (devices, CAP * devices), 1)
    source = lax.broadcasted_iota(jnp.int32, (devices, CAP * devices), 0)
    inbox = jnp.broadcast_to(inbox_ref[...], (devices, CAP * devices)).astype(F32)
    number = lax.broadcasted_iota(jnp.int32, (devices, districts), 1)
    tables = []
    for k in range(CAP):
        wanted = jnp.sum(jnp.where(place == CAP * source + k, inbox, 0.0), axis=1, keepdims=True)
        wanted = jnp.broadcast_to(wanted.astype(jnp.int32), (devices, districts))
        tables.append(jnp.where(wanted == number, 1.0, 0.0))

    others = pl.ds(0, devices - 1)
    whole_a = pltpu.make_async_remote_copy(
        src_ref=send_a.at[others], dst_ref=recv_a.at[others], send_sem=a_send, recv_sem=a_recv,
        device_id=somewhere, device_id_type=MESH,
    )
    whole_a.wait_recv()
    turned = recv_a[...].reshape(devices, LANES).T
    held = jnp.zeros((channels, districts), F32)
    for k in range(CAP):
        held = held + jnp.dot(
            turned[64 * k : 64 * k + channels], tables[k], precision=HIGHEST, preferred_element_type=F32
        )
    resid = held * ((districts / (rows * cols)) ** 0.5) - obs_ref[...]
    resid_ref[...] = resid

    give = jnp.zeros((devices, LANES), F32)
    for k in range(CAP):
        parts = [resid, jnp.zeros((LANES - channels - 64 * k, districts), F32)]
        if k > 0:
            parts = [jnp.zeros((64 * k, districts), F32)] + parts
        give = give + lax.dot_general(
            tables[k], jnp.concatenate(parts, axis=0), NT, precision=HIGHEST, preferred_element_type=F32
        )
    send_b[...] = give.reshape(devices, 1, LANES)
    for ea in range(lat_count + 2):
        for eb in range(lon_count + 2):
            real = min(max(ea - 1, 0), lat_count - 1)
            shift = half if real != ea - 1 else 0
            padded[ea, eb] = send_b[real * lon_count + (eb - 1 + shift) % lon_count]

    def hand_back(i, _):
        to = lax.rem(me + i, devices)
        a, b = coords(to)
        pltpu.make_async_remote_copy(
            src_ref=padded.at[pl.ds(a, 3), pl.ds(b, 3)], dst_ref=recv_b.at[me],
            send_sem=b_send, recv_sem=b_recv, device_id=(a, b), device_id_type=MESH,
        ).start()
        return 0

    lax.fori_loop(1, devices, hand_back, 0)
    recv_b[me] = padded[pl.ds(la, 3), pl.ds(lo, 3)]
    whole_b = pltpu.make_async_remote_copy(
        src_ref=recv_b.at[others], dst_ref=recv_b.at[others], send_sem=b_send, recv_sem=b_recv,
        device_id=somewhere, device_id_type=MESH,
    )
    whole_b.wait_recv()
    nb_ref[...] = recv_b[...]
    whole_a.wait_send()
    whole_b.wait_send()


def adjoint_kernel(
    lat_count, lon_count,
    nb_ref, srows_ref, sstrip_ref, scorner_ref, slot_ref, lat_ref, lon_ref, damp_ref, where_ref,
    out_ref,
    buf_a, buf_b, tbuf_0, tbuf_1, tbuf_2, lonw, latw, mixers, strips, corners,
):
    devices = lat_count * lon_count
    channels, rows, cols = out_ref.shape
    layers = damp_ref.shape[0]
    la = where_ref[0]
    fill_taps(lat_ref, lon_ref, damp_ref, lonw, latw, la, lat_count, True)
    for v in range(3):
        for h in range(3):
            turned = nb_ref[:, v, h, 0, :].T
            wide = jnp.concatenate([turned[0:channels], turned[64 : 64 + channels]], axis=1)
            mixers[v, h] = stacked(wide, 96)

    def mix(mixer, hot):
        made = jnp.dot(mixer, hot, preferred_element_type=F32)
        return made[0:channels] + made[32 : 32 + channels] + made[64 : 64 + channels]

    ids_strip = slot_ids(devices, LANES)
    for h in range(2):
        for p in range(rows // GROUP):
            strips[h, p] = mix(mixers[1, 2 * h], one_hot(sstrip_ref[h, p, 0:1, :].astype(jnp.int32), ids_strip))
        for v in range(2):
            corners[v, h] = mix(
                mixers[2 * v, 2 * h], one_hot(scorner_ref[v, h, 0:1, :].astype(jnp.int32), ids_strip)
            )
    ids = slot_ids(devices, cols)

    def own(i, _):
        made = [mix(mixers[1, 1], one_hot(slot_ref[pl.ds(4 * i + j, 1), :], ids)) for j in range(4)]
        for j in range(4):
            buf_a[HALO + 4 * i + j, :, 0:cols] = made[j]
        return 0

    lax.fori_loop(0, rows // 4, own, 0)

    def ghost(e, _):
        for v in range(2):
            polar = (la == 0) if v == 0 else (la == lat_count - 1)
            row = jnp.where(polar, HALO - 1 - e, e)
            buf_a[e + v * (HALO + rows), :, 0:cols] = mix(
                mixers[2 * v, 1], one_hot(srows_ref[v, pl.ds(row, 1), :], ids)
            )
        return 0

    lax.fori_loop(0, HALO, ghost, 0)
    unpack_rows(
        buf_a, lambda p: strips[1, p], lambda p: strips[0, p], lambda v, h: corners[v, h],
        la, lat_count, rows,
    )
    done = run_passes((buf_a, buf_b), (tbuf_0, tbuf_1, tbuf_2), lonw, latw, layers, rows, True)

    def turn(j, _):
        block = done[pl.ds(HALO + j * 8, 8), :, 0:cols]
        out_ref[:, pl.ds(pl.multiple_of(j * 8, 8), 8), :] = jnp.swapaxes(block, 0, 1)
        return 0

    lax.fori_loop(0, rows // 8, turn, 0)


def local(night_field, lat_kernel, lon_kernel, damping, observed, pixel_slot, inbox_district):
    channels, rows, cols = night_field.shape
    layers = damping.shape[0]
    lat_count, lon_count = lax.axis_size("lat"), lax.axis_size("lon")
    devices = lat_count * lon_count
    districts = observed.shape[1]
    tiles = rows // GROUP
    ext = (rows + 2 * HALO, channels, cols + LANES)
    sums = [pltpu.VMEM((ext[0], 8, ext[2]), F32)] * 3
    vmem = pl.BlockSpec(memory_space=pltpu.VMEM)
    shape = jax.ShapeDtypeStruct
    taps = [pltpu.VMEM((5, channels, LANES), F32), pltpu.VMEM((layers, 3, 5, channels, LANES), F32)]
    sem = pltpu.SemaphoreType.DMA
    residual, nb, srows, sstrip, scorner = pl.pallas_call(
        functools.partial(forward_kernel, lat_count, lon_count),
        out_shape=(
            shape((channels, districts), F32),
            shape((devices, 3, 3, 1, LANES), F32),
            shape((2, HALO, cols), jnp.int32),
            shape((2, tiles, 8, LANES), F32),
            shape((2, 2, 8, LANES), F32),
        ),
        in_specs=[vmem] * 7,
        out_specs=(vmem,) * 5,
        scratch_shapes=[
            pltpu.VMEM(ext, F32),
            pltpu.VMEM(ext, F32),
            *sums,
            *taps,
            pltpu.VMEM((2, tiles, channels + 8, LANES), F32),
            pltpu.VMEM((2, HALO, channels, cols), F32),
            pltpu.VMEM((2, HALO, cols), jnp.int32),
            pltpu.VMEM((2, tiles, channels + 8, LANES), F32),
            pltpu.VMEM((2, 2, channels + 8, LANES), F32),
            pltpu.VMEM((devices, 1, LANES), F32),
            pltpu.VMEM((devices, 1, LANES), F32),
            pltpu.VMEM((devices, 1, LANES), F32),
            pltpu.VMEM((devices, 3, 3, 1, LANES), F32),
            pltpu.VMEM((lat_count + 2, lon_count + 2, 1, LANES), F32),
            sem((10,)), sem((10,)), sem, sem, sem, sem,
        ],
        compiler_params=pltpu.CompilerParams(collective_id=0, has_side_effects=True),
    )(night_field, lat_kernel.T, lon_kernel.T, damping, observed, pixel_slot, inbox_district)
    here = lax.axis_index("lat").reshape(1).astype(jnp.int32)
    back_field = pl.pallas_call(
        functools.partial(adjoint_kernel, lat_count, lon_count),
        out_shape=shape((channels, rows, cols), F32),
        in_specs=[vmem] * 8 + [pl.BlockSpec(memory_space=pltpu.SMEM)],
        out_specs=vmem,
        scratch_shapes=[
            pltpu.VMEM(ext, F32),
            pltpu.VMEM(ext, F32),
            *sums,
            *taps,
            pltpu.VMEM((3, 3, 96, CAP * devices), BF16),
            pltpu.VMEM((2, tiles, channels, LANES), F32),
            pltpu.VMEM((2, 2, channels, LANES), F32),
        ],
    )(nb, srows, sstrip, scorner, pixel_slot, lat_kernel.T, lon_kernel.T, damping, here)
    return back_field, residual


def solution(mesh):
    placed = (
        P(None, "lat", "lon"),
        P(),
        P(),
        P(),
        P(None, ("lat", "lon")),
        P("lat", "lon"),
        P(("lat", "lon"), None),
    )
    return jax.shard_map(
        local,
        mesh=mesh,
        in_specs=placed,
        out_specs=(P(None, "lat", "lon"), P(None, ("lat", "lon"))),
        check_vma=False,
    )
```
